32 devices in a mesh: req: 4 (over y, core), seq: 8 (over z, x).
Axes of the slice: x: 2, y: 2, z: 4, core: 2. Of those that a mesh axis runs over, the one named last changes fastest.
Arguments:
- latent_cache: bfloat16 [4, 4096, 576], P('req', 'seq'), may hold values from -16 to 16
- queries: bfloat16 [4, 3, 128, 576], P('req', None, 'seq'), may hold values from -16 to 16
- chosen: int32 [4, 3, 32], P('req'), may hold values from 0 to 63, as said below
- position: int32 [4], P('req'), may hold values from 4033 to 4096
- w_value: bfloat16 [128, 512, 128], P('seq'), may hold values from -1.5 to 1.5
- w_out: bfloat16 [16384, 7168], P('seq', 'req'), may hold values from -0.0625 to 0.0625
Outputs:
- mixed_out: bfloat16 [7168, 12], P(('req', 'seq'))
The draws below stay inside these ranges and needn't reach their ends.
Inputs may be any that keep to these rules, and one draw needn't show every extreme that they name: `chosen`: block b holds positions b * 64 to b * 64 + 63, which lie on shard b // 8 of seq. A query's 32 numbers are distinct; at most 8 of them lie on one shard and exactly 8 on some shard, for every query; every query names the last block; its blocks on the other shards are spread as evenly as possible over those shards.
All inputs are finite; a program needn't handle non-finite values.
Results may differ from the reference program's by a relative error of at most 0.013.
Values may be sent and summed in bfloat16 or wider, within the bound.
A program may use at most 128 MiB of HBM per device.

```python
import math
import jax
import jax.numpy as jnp
from jax import lax

HEADS = 128
LATENT = 512
ROPE = 64
VDIM = 128
D = 7168
BLOCK = 64
TOPB = 32
MAXB = 8
BLOCKS_DEV = 8
STEPS = 3
REQUESTS = 4
SEQLEN = 4096
N_SEQ = 8


def shuffled_row(row_key):
    return jax.random.permutation(row_key, BLOCKS_DEV).astype(jnp.int32)


def shuffled_short(row_key):
    return jax.random.permutation(row_key, BLOCKS_DEV - 1).astype(jnp.int32)


def one_query(key):
    others = TOPB - MAXB
    last_shard = N_SEQ - 1
    hot_shard = jax.random.randint(jax.random.fold_in(key, 1), (), 0, N_SEQ).astype(jnp.int32)
    spread_hot = jax.random.permutation(jax.random.fold_in(key, 2), BLOCKS_DEV)[:MAXB].astype(jnp.int32)
    tail_hot = jnp.concatenate([jnp.full((1,), BLOCKS_DEV - 1, jnp.int32), jax.random.permutation(jax.random.fold_in(key, 3), BLOCKS_DEV - 1)[:MAXB - 1].astype(jnp.int32)])
    hot_pick = jnp.where(hot_shard == last_shard, tail_hot, spread_hot)
    other_order = ((hot_shard + 1 + jax.random.permutation(jax.random.fold_in(key, 4), N_SEQ - 1)) % N_SEQ).astype(jnp.int32)
    leading = other_order[0]
    swapped = jnp.where(other_order == last_shard, leading, other_order)
    swapped = swapped.at[0].set(last_shard)
    other_order = jnp.where(hot_shard == last_shard, other_order, swapped)
    item_index = jnp.arange(others, dtype=jnp.int32)
    shard_ids = other_order[item_index % (N_SEQ - 1)]
    depth = item_index // (N_SEQ - 1)
    table_keys = jax.random.split(jax.random.fold_in(key, 5), N_SEQ)
    full_rows = jax.vmap(shuffled_row)(table_keys)
    tail_rows = jnp.concatenate([jnp.full((N_SEQ, 1), BLOCKS_DEV - 1, jnp.int32), jax.vmap(shuffled_short)(table_keys)], axis=1)
    row_is_last = (jnp.arange(N_SEQ, dtype=jnp.int32) == last_shard)[:, None]
    offsets_table = jnp.where(row_is_last, tail_rows, full_rows)
    other_blocks = shard_ids * BLOCKS_DEV + offsets_table[shard_ids, depth]
    blocks = jnp.concatenate([hot_shard * BLOCKS_DEV + hot_pick, other_blocks])
    return blocks[jax.random.permutation(jax.random.fold_in(key, 6), TOPB)]


def draw_chosen(key, part):
    query_keys = jax.random.split(jax.random.fold_in(key, 17), REQUESTS * STEPS)
    blocks = jax.vmap(one_query)(query_keys)
    return blocks.reshape(REQUESTS, STEPS, TOPB).astype(jnp.int32)


def draw_latent_cache(key, part):
    base = jax.random.fold_in(key, 31)
    shape = (REQUESTS, SEQLEN, LATENT + ROPE)
    values = jax.random.normal(base, shape, jnp.float32)
    return jnp.clip(values, -16.0, 16.0).astype(jnp.bfloat16)


def draw_queries(key, part):
    base = jax.random.fold_in(key, 47)
    shape = (REQUESTS, STEPS, HEADS, LATENT + ROPE)
    row_scale = jnp.exp(jax.random.uniform(jax.random.fold_in(key, 48), (REQUESTS, STEPS, HEADS, 1), jnp.float32, math.log(0.5), math.log(2.0)))
    values = jax.random.normal(base, shape, jnp.float32) * row_scale
    return jnp.clip(values, -16.0, 16.0).astype(jnp.bfloat16)


def set_ends(result, own_key, low, largest):
    longest = result.shape.index(max(result.shape))
    spots = []
    for shift in (0, 1):
        where = [jax.random.randint(jax.random.fold_in(own_key, axis), (), 0, length) for axis, length in enumerate(result.shape)]
        where[longest] = (where[longest] + shift) % result.shape[longest]
        spots.append(tuple(where))
    return result.at[spots[0]].set(low).at[spots[1]].set(largest)


def with_spikes(values, stream_key, source, target, parts, factor):
    def block_of(dim):
        return (jnp.arange(values.shape[dim]) // (values.shape[dim] // parts)).reshape((-1,) + (1,) * (values.ndim - 1 - dim))

    near = jax.random.permutation(stream_key, parts)[block_of(target)]
    far = (block_of(target) + parts // 2) % parts
    return jnp.where((block_of(source) == near) | (block_of(source) == far), factor * values, values)


def steps_of(key, shape, cuts, smallest, largest):
    def one(axis_at, parts):
        draws = jax.random.uniform(jax.random.fold_in(jax.random.fold_in(key, 6), axis_at), (parts,), jnp.float32, smallest / len(cuts), largest / len(cuts))
        return jnp.repeat(jnp.exp(draws), shape[axis_at] // parts).reshape((-1,) + (1,) * (len(shape) - axis_at - 1))

    level = one(*cuts[0])
    for cut in cuts[1:]:
        level = level * one(*cut)
    return level


def gaussian(stream_key, shape, width, bound, cuts=(), kind=jnp.bfloat16):
    drawn = width * jax.random.normal(stream_key, shape, jnp.float32)
    if cuts:
        drawn = drawn * steps_of(stream_key, shape, cuts, -0.22, 0.18)
    return jnp.clip(drawn, -bound, bound).astype(kind)


def noise_with(key, dims, width, most, pieces, heavy, held_as=jnp.bfloat16):
    array = width * jax.random.normal(key, dims, jnp.float32)
    if pieces:
        array = array * steps_of(key, dims, pieces, -0.22, 0.18)
    return jnp.clip(with_spikes(array, jax.random.fold_in(key, 3), *heavy), -most, most).astype(held_as)


def setup_inputs(seed: int = 0) -> dict:
    key_of = jax.random.split(jax.random.key(seed), 7)
    latent_cache = draw_latent_cache(jax.random.fold_in(key_of[6], 71), 0)
    queries = draw_queries(jax.random.fold_in(key_of[6], 71), 0)
    chosen = draw_chosen(jax.random.fold_in(key_of[6], 71), 0)
    position = set_ends(jax.random.randint(key_of[3], (REQUESTS,), SEQLEN - BLOCK + 1, SEQLEN + 1), jax.random.fold_in(key_of[3], 1), SEQLEN - BLOCK + 1, SEQLEN).astype(jnp.int32)
    w_value = gaussian(key_of[4], (HEADS, LATENT, VDIM), 16 ** -0.5, 1.5, ((0, 8),))
    w_out = noise_with(key_of[5], (HEADS * VDIM, D), (HEADS * VDIM) ** -0.5, 0.0625, ((0, 8), (1, 4)), (0, 1, 8, 2.0))
    return dict(latent_cache=latent_cache, queries=queries, chosen=chosen, position=position, w_value=w_value, w_out=w_out)


score_scale = 1.0 / math.sqrt(192.0)
very_low = -1e+30

def attend(query_rows, gathered, usable):
    query_wide = query_rows.astype(jnp.float32)
    gathered_wide = gathered.astype(jnp.float32)
    scores = jnp.dot(query_wide, gathered_wide.T, precision=lax.Precision.HIGHEST, preferred_element_type=jnp.float32) * score_scale
    scores = jnp.where(usable[None, :], scores, very_low)
    row_peak = lax.optimization_barrier(jnp.max(scores, axis=1, keepdims=True))
    raw_weights = jnp.where(usable[None, :], jnp.exp(scores - row_peak), 0.0)
    row_total = lax.optimization_barrier(jnp.sum(raw_weights, axis=1, keepdims=True))
    rounded = lax.optimization_barrier(raw_weights.astype(jnp.bfloat16))
    weighted = jnp.dot(rounded.astype(jnp.float32), gathered_wide[:, :LATENT], precision=lax.Precision.HIGHEST, preferred_element_type=jnp.float32)
    return (weighted / row_total).astype(jnp.bfloat16)

def reference(latent_cache, queries, chosen, position, w_value, w_out):
    inside = jnp.arange(BLOCK, dtype=jnp.int32)
    value_wide = w_value.astype(jnp.float32)

    def per_request(request):
        request_cache = latent_cache[request]
        per_step = []
        for decode_step in range(STEPS):
            token_ids = (chosen[request, decode_step][:, None] * BLOCK + inside[None, :]).reshape(-1)
            gathered = jnp.take(request_cache, token_ids, axis=0)
            usable = token_ids < position[request]
            latent_out = attend(queries[request, decode_step], gathered, usable)
            head_rows = jnp.einsum('hl,hlv->hv', latent_out.astype(jnp.float32), value_wide, precision=lax.Precision.HIGHEST).astype(jnp.bfloat16)
            per_step.append(head_rows.reshape(-1))
        return jnp.stack(per_step)
    head_out = lax.map(per_request, jnp.arange(REQUESTS, dtype=jnp.int32))
    head_out = lax.optimization_barrier(head_out)
    head_wide = head_out.reshape(REQUESTS * STEPS, HEADS * VDIM).astype(jnp.float32)
    mixed_out = jnp.dot(head_wide, w_out.astype(jnp.float32), precision=lax.Precision.HIGHEST, preferred_element_type=jnp.float32)
    return mixed_out.T.astype(jnp.bfloat16)
```

```python
import functools
import math

import jax
import jax.numpy as jnp
from jax import lax
from jax.experimental import pallas as pl
from jax.experimental.pallas import tpu as pltpu
from jax.sharding import PartitionSpec as P

LATENT = 512
BLOCK = 64
LANES = 128
STATS = 128
MESH = pl.DeviceIdType.MESH

score_scale = 1.0 / math.sqrt(192.0)
very_low = -1e30


def kernel(
    n_seq, n_req, steps, heads,
    chosen_ref, position_ref, q_hbm, cache_hbm, wv_hbm, wo_hbm,
    out_ref,
    qbuf, cache, wv, wo, mask, part, got, lat, hf, hsend, hall, hwide, ysend, yrecv,
    load_sem, q_send, q_recv, p_send, p_recv, h_send, h_recv, y_send, y_recv,
):
    me = lax.axis_index("seq")
    req = lax.axis_index("req")
    rows = steps * heads
    cache_len = cache.shape[0]
    cols = ysend.shape[2]

    loads = [
        pltpu.make_async_copy(q_hbm, qbuf.at[0], load_sem.at[0]),
        pltpu.make_async_copy(cache_hbm, cache, load_sem.at[1]),
        pltpu.make_async_copy(wv_hbm, wv, load_sem.at[2]),
        pltpu.make_async_copy(wo_hbm, wo, load_sem.at[3]),
    ]
    loads[0].start()
    loads[1].start()

    def seq_at(offset):
        return {"seq": lax.rem(me + offset + n_seq, n_seq)}

    def req_at(offset):
        return {"req": lax.rem(req + offset + n_req, n_req)}

    barrier = pltpu.get_barrier_semaphore()
    for d in range(1, n_seq):
        pl.semaphore_signal(barrier, inc=1, device_id=seq_at(d), device_id_type=MESH)
    for e in range(1, n_req):
        pl.semaphore_signal(barrier, inc=1, device_id=req_at(e), device_id_type=MESH)
    pl.semaphore_wait(barrier, n_seq + n_req - 2)

    def query_copy(d):
        return pltpu.make_async_remote_copy(
            src_ref=q_hbm, dst_ref=qbuf.at[d], send_sem=q_send.at[d], recv_sem=q_recv.at[d],
            device_id=seq_at(d), device_id_type=MESH,
        )

    def part_copy(d):
        return pltpu.make_async_remote_copy(
            src_ref=part.at[d], dst_ref=got.at[d], send_sem=p_send.at[d], recv_sem=p_recv.at[d],
            device_id=seq_at(-d), device_id_type=MESH,
        )

    def head_copy(e):
        return pltpu.make_async_remote_copy(
            src_ref=hsend, dst_ref=hall.at[req], send_sem=h_send.at[e], recv_sem=h_recv.at[e],
            device_id=req_at(e), device_id_type=MESH,
        )

    def out_copy(d):
        return pltpu.make_async_remote_copy(
            src_ref=ysend.at[lax.rem(me + d, n_seq)], dst_ref=yrecv.at[d],
            send_sem=y_send.at[d], recv_sem=y_recv.at[d],
            device_id=seq_at(d), device_id_type=MESH,
        )

    order = sorted(range(1, n_seq), key=lambda d: (min(d, n_seq - d), d))
    for d in order:
        query_copy(d).start()
    loads[2].start()
    loads[3].start()

    block = me * (cache_len // BLOCK) + lax.broadcasted_iota(jnp.int32, (1, cache_len), 1) // BLOCK
    inside = me * cache_len + lax.broadcasted_iota(jnp.int32, (1, cache_len), 1) < position_ref[0]
    row_step = lax.broadcasted_iota(jnp.int32, (rows, cache_len), 0) // heads
    usable = jnp.zeros((rows, cache_len), jnp.float32)
    for t in range(steps):
        named = block == chosen_ref[t, 0]
        for k in range(1, chosen_ref.shape[1]):
            named = named | (block == chosen_ref[t, k])
        flag = jnp.where(named & inside, 1.0, 0.0)
        usable = jnp.where(row_step == t, flag, usable)
    mask[...] = usable
    loads[0].wait()
    loads[1].wait()

    def attend(d):
        keep = mask[...] > 0.0
        scores = lax.dot_general(
            qbuf[d], cache[...], (((1,), (1,)), ((), ())), preferred_element_type=jnp.float32
        ) * score_scale
        scores = jnp.where(keep, scores, very_low)
        peak = jnp.max(scores, axis=1, keepdims=True).astype(jnp.bfloat16).astype(jnp.float32)
        raw = jnp.where(keep, jnp.exp(scores - peak), 0.0)
        total = jnp.sum(raw, axis=1, keepdims=True)
        summed = jnp.dot(
            raw.astype(jnp.bfloat16), cache[:, :LATENT], preferred_element_type=jnp.float32
        )
        high = total.astype(jnp.bfloat16).astype(jnp.float32)
        lane = lax.broadcasted_iota(jnp.int32, (rows, STATS), 1)
        stats = jnp.where(lane == 0, peak, jnp.where(lane == 1, high, total - high))
        part[d, :, :LATENT] = summed.astype(jnp.bfloat16)
        part[d, :, LATENT:] = stats.astype(jnp.bfloat16)

    def answer(d):
        query_copy(d).wait_recv()
        attend(d)
        part_copy(d).start()

    if n_seq <= 8:
        for d in order:
            answer(d)
        attend(0)
    else:
        pl.loop(1, n_seq)(answer)
        attend(0)

    def parts_of(ref, d):
        stats = ref[d, :, LATENT:].astype(jnp.float32)
        return (
            stats[:, 0:1], stats[:, 1:2] + stats[:, 2:3], ref[d, :, :LATENT].astype(jnp.float32)
        )

    def join(left, right):
        peak = jnp.maximum(left[0], right[0])
        scale_left = jnp.exp(left[0] - peak)
        scale_right = jnp.exp(right[0] - peak)
        return (
            peak,
            left[1] * scale_left + right[1] * scale_right,
            left[2] * scale_left + right[2] * scale_right,
        )

    def take(d, running):
        part_copy(d).wait_recv()
        return join(running, parts_of(got, d))

    running = parts_of(part, 0)
    if n_seq <= 8:
        for d in order:
            running = take(d, running)
    else:
        running = lax.fori_loop(1, n_seq, take, running)
    latent_out = (running[2] / running[1]).astype(jnp.bfloat16).astype(jnp.float32)
    for c in range(LATENT // LANES):
        lat[c] = latent_out[:, c * LANES:(c + 1) * LANES]

    loads[2].wait()
    for h in range(heads):
        pick = pl.ds(h, steps, stride=heads)
        row = jnp.concatenate([lat[c, pick, :] for c in range(LATENT // LANES)], axis=1)
        hf[pick, :] = jnp.dot(
            row.astype(jnp.bfloat16), wv[h], preferred_element_type=jnp.float32
        )
    hsend[...] = hf[...].astype(jnp.bfloat16)
    for e in range(1, n_req):
        head_copy(e).start()
    hall[req] = hsend[...]
    for e in range(1, n_req):
        head_copy(e).wait_recv()
    for r in range(n_req):
        hwide[r * rows:(r + 1) * rows, :] = hall[r].astype(jnp.float32)
    flat = jnp.concatenate(
        [hwide[pl.ds(h, n_req * steps, stride=heads), :] for h in range(heads)], axis=1
    ).astype(jnp.bfloat16)

    loads[3].wait()
    mixed = jnp.dot(flat, wo[...], preferred_element_type=jnp.float32)
    for j in range(n_seq):
        ysend[j] = mixed[:, j * cols:(j + 1) * cols]
    for d in order:
        out_copy(d).start()
    total = ysend[me]
    for d in order:
        out_copy(d).wait_recv()
        total = total + yrecv[d]
    out_ref[...] = total.T.astype(out_ref.dtype)

    for d in order:
        query_copy(d).wait_send()
        part_copy(d).wait_send()
        out_copy(d).wait_send()
    for e in range(1, n_req):
        head_copy(e).wait_send()


def body(n_seq, n_req, latent_cache, queries, chosen, position, w_value, w_out):
    req_dev, cache_len, width = latent_cache.shape
    assert req_dev == 1
    steps, heads = queries.shape[1], queries.shape[2]
    rows = steps * heads
    vdim = w_value.shape[2]
    cols = w_out.shape[1] // n_seq
    bf16, f32 = jnp.bfloat16, jnp.float32
    everywhere = pl.BlockSpec(memory_space=pl.ANY)
    scalars = pl.BlockSpec(memory_space=pltpu.SMEM)
    dma = pltpu.SemaphoreType.DMA
    return pl.pallas_call(
        functools.partial(kernel, n_seq, n_req, steps, heads),
        out_shape=jax.ShapeDtypeStruct((cols, n_req * steps), bf16),
        in_specs=[scalars, scalars] + [everywhere] * 4,
        out_specs=pl.BlockSpec(memory_space=pltpu.VMEM),
        scratch_shapes=[
            pltpu.VMEM((n_seq, rows, width), bf16),
            pltpu.VMEM((cache_len, width), bf16),
            pltpu.VMEM(w_value.shape, bf16),
            pltpu.VMEM(w_out.shape, bf16),
            pltpu.VMEM((rows, cache_len), f32),
            pltpu.VMEM((n_seq, rows, LATENT + STATS), bf16),
            pltpu.VMEM((n_seq, rows, LATENT + STATS), bf16),
            pltpu.VMEM((LATENT // LANES, rows, LANES), f32),
            pltpu.VMEM((rows, vdim), f32),
            pltpu.VMEM((rows, vdim), bf16),
            pltpu.VMEM((n_req, rows, vdim), bf16),
            pltpu.VMEM((n_req * rows, vdim), f32),
            pltpu.VMEM((n_seq, n_req * steps, cols), f32),
            pltpu.VMEM((n_seq, n_req * steps, cols), f32),
            dma((4,)),
            dma((n_seq,)), dma((n_seq,)), dma((n_seq,)), dma((n_seq,)),
            dma((n_req,)), dma((n_req,)), dma((n_seq,)), dma((n_seq,)),
        ],
        compiler_params=pltpu.CompilerParams(
            collective_id=0, has_side_effects=True, vmem_limit_bytes=60 << 20
        ),
    )(
        chosen.reshape(steps, chosen.shape[2]),
        position,
        queries.reshape(rows, width),
        latent_cache.reshape(cache_len, width),
        w_value,
        w_out,
    )


def solution(mesh):
    return jax.shard_map(
        functools.partial(body, mesh.shape["seq"], mesh.shape["req"]),
        mesh=mesh,
        in_specs=(
            P("req", "seq", None),
            P("req", None, "seq", None),
            P("req", None, None),
            P("req"),
            P("seq", None, None),
            P("seq", "req"),
        ),
        out_specs=P(("req", "seq"), None),
        check_vma=False,
    )
```

```python
import functools
import math

import jax
import jax.numpy as jnp
from jax import lax
from jax.experimental import pallas as pl
from jax.experimental.pallas import tpu as pltpu
from jax.sharding import PartitionSpec as P

LATENT = 512
BLOCK = 64
LANES = 128
STATS = 128
MESH = pl.DeviceIdType.MESH

score_scale = 1.0 / math.sqrt(192.0)
very_low = -1e30


def kernel(
    n_seq, n_req, steps, heads,
    chosen_ref, position_ref, q_hbm, cache_hbm, wv_hbm, wo_hbm,
    out_ref,
    qbuf, cache, wv, wo, mask, part, got, lat, hf, hsend, hall, hwide, ysend, yrecv,
    load_sem, q_send, q_recv, p_send, p_recv, h_send, h_recv, y_send, y_recv,
):
    me = lax.axis_index("seq")
    req = lax.axis_index("req")
    rows = steps * heads
    cache_len = cache.shape[1]
    cols = ysend.shape[2]

    loads = [
        pltpu.make_async_copy(q_hbm, qbuf.at[0], load_sem.at[0]),
        pltpu.make_async_copy(cache_hbm, cache, load_sem.at[1]),
        pltpu.make_async_copy(wv_hbm, wv, load_sem.at[2]),
        pltpu.make_async_copy(wo_hbm, wo, load_sem.at[3]),
    ]
    loads[0].start()
    loads[1].start()

    def seq_at(offset):
        return {"seq": lax.rem(me + offset + n_seq, n_seq)}

    def req_at(offset):
        return {"req": lax.rem(req + offset + n_req, n_req)}

    barrier = pltpu.get_barrier_semaphore()
    for d in range(1, n_seq):
        pl.semaphore_signal(barrier, inc=1, device_id=seq_at(d), device_id_type=MESH)
    for e in range(1, n_req):
        pl.semaphore_signal(barrier, inc=1, device_id=req_at(e), device_id_type=MESH)
    pl.semaphore_wait(barrier, n_seq + n_req - 2)

    def query_copy(d):
        return pltpu.make_async_remote_copy(
            src_ref=q_hbm, dst_ref=qbuf.at[d], send_sem=q_send.at[d], recv_sem=q_recv.at[d],
            device_id=seq_at(d), device_id_type=MESH,
        )

    def part_copy(d):
        return pltpu.make_async_remote_copy(
            src_ref=part.at[d], dst_ref=got.at[d], send_sem=p_send.at[d], recv_sem=p_recv.at[d],
            device_id=seq_at(-d), device_id_type=MESH,
        )

    def head_copy(e):
        return pltpu.make_async_remote_copy(
            src_ref=hsend, dst_ref=hall.at[req], send_sem=h_send.at[e], recv_sem=h_recv.at[e],
            device_id=req_at(e), device_id_type=MESH,
        )

    def out_copy(d):
        return pltpu.make_async_remote_copy(
            src_ref=ysend.at[lax.rem(me + d, n_seq)], dst_ref=yrecv.at[d],
            send_sem=y_send.at[d], recv_sem=y_recv.at[d],
            device_id=seq_at(d), device_id_type=MESH,
        )

    order = sorted(range(1, n_seq), key=lambda d: (min(d, n_seq - d), d))
    for d in order:
        query_copy(d).start()
    loads[2].start()
    loads[3].start()

    block = me * (cache_len // BLOCK) + lax.broadcasted_iota(jnp.int32, (1, cache_len), 1) // BLOCK
    inside = me * cache_len + lax.broadcasted_iota(jnp.int32, (1, cache_len), 1) < position_ref[0]
    row_step = lax.broadcasted_iota(jnp.int32, (rows, cache_len), 0) // heads
    usable = jnp.zeros((rows, cache_len), jnp.float32)
    for t in range(steps):
        named = block == chosen_ref[t, 0, 0]
        for k in range(1, chosen_ref.shape[2]):
            named = named | (block == chosen_ref[t, 0, k])
        flag = jnp.where(named & inside, 1.0, 0.0)
        usable = jnp.where(row_step == t, flag, usable)
    mask[...] = usable
    loads[0].wait()
    loads[1].wait()

    def attend(d):
        keep = mask[...] > 0.0
        scores = lax.dot_general(
            qbuf[d], cache[...], (((1,), (0,)), ((), ())), preferred_element_type=jnp.float32
        ) * score_scale
        scores = jnp.where(keep, scores, very_low)
        peak = jnp.max(scores, axis=1, keepdims=True).astype(jnp.bfloat16).astype(jnp.float32)
        raw = jnp.where(keep, jnp.exp(scores - peak), 0.0)
        total = jnp.sum(raw, axis=1, keepdims=True)
        summed = lax.dot_general(
            raw.astype(jnp.bfloat16), cache[:LATENT, :], (((1,), (1,)), ((), ())),
            preferred_element_type=jnp.float32,
        )
        high = total.astype(jnp.bfloat16).astype(jnp.float32)
        lane = lax.broadcasted_iota(jnp.int32, (rows, STATS), 1)
        stats = jnp.where(lane == 0, peak, jnp.where(lane == 1, high, total - high))
        part[d, :, :LATENT] = summed.astype(jnp.bfloat16)
        part[d, :, LATENT:] = stats.astype(jnp.bfloat16)

    def answer(d):
        query_copy(d).wait_recv()
        attend(d)
        part_copy(d).start()

    if n_seq <= 8:
        for d in order:
            answer(d)
        attend(0)
    else:
        pl.loop(1, n_seq)(answer)
        attend(0)

    def parts_of(ref, d):
        stats = ref[d, :, LATENT:].astype(jnp.float32)
        return (
            stats[:, 0:1], stats[:, 1:2] + stats[:, 2:3], ref[d, :, :LATENT].astype(jnp.float32)
        )

    def join(left, right):
        peak = jnp.maximum(left[0], right[0])
        scale_left = jnp.exp(left[0] - peak)
        scale_right = jnp.exp(right[0] - peak)
        return (
            peak,
            left[1] * scale_left + right[1] * scale_right,
            left[2] * scale_left + right[2] * scale_right,
        )

    def take(d, running):
        part_copy(d).wait_recv()
        return join(running, parts_of(got, d))

    running = parts_of(part, 0)
    if n_seq <= 8:
        for d in order:
            running = take(d, running)
    else:
        running = lax.fori_loop(1, n_seq, take, running)
    latent_out = (running[2] / running[1]).astype(jnp.bfloat16).astype(jnp.float32)
    for c in range(LATENT // LANES):
        lat[c] = latent_out[:, c * LANES:(c + 1) * LANES]

    loads[2].wait()
    for h in range(heads):
        pick = pl.ds(h, steps, stride=heads)
        row = jnp.concatenate([lat[c, pick, :] for c in range(LATENT // LANES)], axis=1)
        hf[pick, :] = jnp.dot(
            row.astype(jnp.bfloat16), wv[h], preferred_element_type=jnp.float32
        )
    hsend[...] = hf[...].astype(jnp.bfloat16)
    for e in range(1, n_req):
        head_copy(e).start()
    hall[req] = hsend[...]
    for e in range(1, n_req):
        head_copy(e).wait_recv()
    for r in range(n_req):
        hwide[r * rows:(r + 1) * rows, :] = hall[r].astype(jnp.float32)
    flat = jnp.concatenate(
        [hwide[pl.ds(h, n_req * steps, stride=heads), :] for h in range(heads)], axis=1
    ).astype(jnp.bfloat16)

    loads[3].wait()
    mixed = jnp.dot(flat, wo[...], preferred_element_type=jnp.float32)
    for j in range(n_seq):
        ysend[j] = mixed[:, j * cols:(j + 1) * cols]
    for d in order:
        out_copy(d).start()
    total = ysend[me]
    for d in order:
        out_copy(d).wait_recv()
        total = total + yrecv[d]
    out_ref[...] = total

    for d in order:
        query_copy(d).wait_send()
        part_copy(d).wait_send()
        out_copy(d).wait_send()
    for e in range(1, n_req):
        head_copy(e).wait_send()


def body(n_seq, n_req, latent_cache, queries, chosen, position, w_value, w_out):
    req_dev, cache_len, width = latent_cache.shape
    assert req_dev == 1
    steps, heads = queries.shape[1], queries.shape[2]
    rows = steps * heads
    vdim = w_value.shape[2]
    cols = w_out.shape[1] // n_seq
    bf16, f32 = jnp.bfloat16, jnp.float32
    everywhere = pl.BlockSpec(memory_space=pl.ANY)
    scalars = pl.BlockSpec(memory_space=pltpu.SMEM)
    dma = pltpu.SemaphoreType.DMA
    mixed_out = pl.pallas_call(
        functools.partial(kernel, n_seq, n_req, steps, heads),
        out_shape=jax.ShapeDtypeStruct((n_req * steps, cols), f32),
        in_specs=[scalars, scalars] + [everywhere] * 4,
        out_specs=pl.BlockSpec(memory_space=pltpu.VMEM),
        scratch_shapes=[
            pltpu.VMEM((n_seq, rows, width), bf16),
            pltpu.VMEM((width, cache_len), bf16),
            pltpu.VMEM(w_value.shape, bf16),
            pltpu.VMEM(w_out.shape, bf16),
            pltpu.VMEM((rows, cache_len), f32),
            pltpu.VMEM((n_seq, rows, LATENT + STATS), bf16),
            pltpu.VMEM((n_seq, rows, LATENT + STATS), bf16),
            pltpu.VMEM((LATENT // LANES, rows, LANES), f32),
            pltpu.VMEM((rows, vdim), f32),
            pltpu.VMEM((rows, vdim), bf16),
            pltpu.VMEM((n_req, rows, vdim), bf16),
            pltpu.VMEM((n_req * rows, vdim), f32),
            pltpu.VMEM((n_seq, n_req * steps, cols), f32),
            pltpu.VMEM((n_seq, n_req * steps, cols), f32),
            dma((4,)),
            dma((n_seq,)), dma((n_seq,)), dma((n_seq,)), dma((n_seq,)),
            dma((n_req,)), dma((n_req,)), dma((n_seq,)), dma((n_seq,)),
        ],
        compiler_params=pltpu.CompilerParams(
            collective_id=0, has_side_effects=True, vmem_limit_bytes=60 << 20
        ),
    )(
        chosen.transpose(1, 0, 2),
        position,
        queries.reshape(rows, width),
        latent_cache.reshape(cache_len, width).T,
        w_value,
        w_out,
    )
    return mixed_out.T.astype(bf16)


def solution(mesh):
    return jax.shard_map(
        functools.partial(body, mesh.shape["seq"], mesh.shape["req"]),
        mesh=mesh,
        in_specs=(
            P("req", "seq", None),
            P("req", None, "seq", None),
            P("req", None, None),
            P("req"),
            P("seq", None, None),
            P("seq", "req"),
        ),
        out_specs=P(("req", "seq"), None),
        check_vma=False,
    )
```

```python
import functools
import math

import jax
import jax.numpy as jnp
from jax import lax
from jax.experimental import pallas as pl
from jax.experimental.pallas import tpu as pltpu
from jax.sharding import PartitionSpec as P

LATENT = 512
BLOCK = 64
LANES = 128
STATS = 128
MESH = pl.DeviceIdType.MESH

score_scale = 1.0 / math.sqrt(192.0)
very_low = -1e30


def kernel(
    n_seq, n_req, steps, heads,
    chosen_ref, position_ref, q_hbm, cache_hbm, wv_hbm, wo_hbm,
    out_ref,
    qbuf, cache, wv, wo, mask, part, pair, joint, got, lat, hf, hsend, hall, hwide, ysend, yrecv,
    load_sem, q_send, q_recv, f_send, f_recv, p_send, p_recv, j_send, j_recv,
    h_send, h_recv, y_send, y_recv,
):
    me = lax.axis_index("seq")
    req = lax.axis_index("req")
    rows = steps * heads
    cache_len = cache.shape[1]
    cols = ysend.shape[2]
    groups = n_seq // 2
    group, side = me // 2, me % 2

    loads = [
        pltpu.make_async_copy(q_hbm, qbuf.at[0, 0], load_sem.at[0]),
        pltpu.make_async_copy(cache_hbm, cache, load_sem.at[1]),
        pltpu.make_async_copy(wv_hbm, wv, load_sem.at[2]),
        pltpu.make_async_copy(wo_hbm, wo, load_sem.at[3]),
    ]
    loads[0].start()
    loads[1].start()

    def seq_at(offset):
        return {"seq": lax.rem(me + offset, n_seq)}

    def req_at(offset):
        return {"req": lax.rem(req + offset, n_req)}

    def column(k):
        other, bit = 0, 1
        while bit < groups:
            own = (group // bit) % 2
            other = other + bit * ((1 - own) if k & bit else own)
            bit *= 2
        return {"seq": 2 * other + side}

    partner = {"seq": 2 * group + 1 - side}

    barrier = pltpu.get_barrier_semaphore()
    for d in range(1, n_seq):
        pl.semaphore_signal(barrier, inc=1, device_id=seq_at(d), device_id_type=MESH)
    for e in range(1, n_req):
        pl.semaphore_signal(barrier, inc=1, device_id=req_at(e), device_id_type=MESH)

    block = me * (cache_len // BLOCK) + lax.broadcasted_iota(jnp.int32, (1, cache_len), 1) // BLOCK
    inside = me * cache_len + lax.broadcasted_iota(jnp.int32, (1, cache_len), 1) < position_ref[0]
    row_step = lax.broadcasted_iota(jnp.int32, (rows, cache_len), 0) // heads
    usable = jnp.zeros((rows, cache_len), jnp.float32)
    for t in range(steps):
        named = block == chosen_ref[t, 0, 0]
        for k in range(1, chosen_ref.shape[2]):
            named = named | (block == chosen_ref[t, 0, k])
        flag = jnp.where(named & inside, 1.0, 0.0)
        usable = jnp.where(row_step == t, flag, usable)
    mask[...] = usable
    pl.semaphore_wait(barrier, n_seq + n_req - 2)

    def remote(src, dst, send, recv, device):
        return pltpu.make_async_remote_copy(
            src_ref=src, dst_ref=dst, send_sem=send, recv_sem=recv,
            device_id=device, device_id_type=MESH,
        )

    def query_copy(k):
        return remote(q_hbm, qbuf.at[k, 0], q_send.at[k], q_recv.at[k], column(k))

    def forward_copy(k):
        src = qbuf.at[k, 0] if k else q_hbm
        return remote(src, qbuf.at[k, 1], f_send.at[k], f_recv.at[k], partner)

    def pair_copy(k):
        return remote(part.at[k, 1], pair.at[k], p_send.at[k], p_recv.at[k], partner)

    def joint_copy(k):
        return remote(joint.at[k], got.at[k], j_send.at[k], j_recv.at[k], column(k))

    def head_copy(e):
        return remote(hsend, hall.at[req], h_send.at[e], h_recv.at[e], req_at(e))

    def out_copy(d):
        return remote(
            ysend.at[lax.rem(me + d, n_seq)], yrecv.at[d], y_send.at[d], y_recv.at[d], seq_at(d)
        )

    order = sorted(range(1, n_seq), key=lambda d: (min(d, n_seq - d), d))
    forward_copy(0).start()
    for k in range(1, groups):
        query_copy(k).start()
    loads[2].start()
    loads[3].start()
    loads[0].wait()
    loads[1].wait()

    def store(ref, at, peak, total, summed):
        high = total.astype(jnp.bfloat16).astype(jnp.float32)
        lane = lax.broadcasted_iota(jnp.int32, (rows, STATS), 1)
        stats = jnp.where(lane == 0, peak, jnp.where(lane == 1, high, total - high))
        ref[at + (slice(None), slice(0, LATENT))] = summed.astype(jnp.bfloat16)
        ref[at + (slice(None), slice(LATENT, LATENT + STATS))] = stats.astype(jnp.bfloat16)

    def load(ref, at):
        stats = ref[at + (slice(None), slice(LATENT, LATENT + STATS))].astype(jnp.float32)
        return (
            stats[:, 0:1],
            stats[:, 1:2] + stats[:, 2:3],
            ref[at + (slice(None), slice(0, LATENT))].astype(jnp.float32),
        )

    def attend(k, j):
        keep = mask[...] > 0.0
        scores = lax.dot_general(
            qbuf[k, j], cache[...], (((1,), (0,)), ((), ())), preferred_element_type=jnp.float32
        ) * score_scale
        scores = jnp.where(keep, scores, very_low)
        peak = jnp.max(scores, axis=1, keepdims=True).astype(jnp.bfloat16).astype(jnp.float32)
        raw = jnp.where(keep, jnp.exp(scores - peak), 0.0)
        total = jnp.sum(raw, axis=1, keepdims=True)
        summed = lax.dot_general(
            raw.astype(jnp.bfloat16), cache[:LATENT, :], (((1,), (1,)), ((), ())),
            preferred_element_type=jnp.float32,
        )
        store(part, (k, j), peak, total, summed)

    def join(left, right):
        peak = jnp.maximum(left[0], right[0])
        scale_left = jnp.exp(left[0] - peak)
        scale_right = jnp.exp(right[0] - peak)
        return (
            peak,
            left[1] * scale_left + right[1] * scale_right,
            left[2] * scale_left + right[2] * scale_right,
        )

    def serve_partner(k):
        forward_copy(k).wait_recv()
        attend(k, 1)
        pair_copy(k).start()

    def joined(k):
        pair_copy(k).wait_recv()
        return join(load(part, (k, 0)), load(pair, (k,)))

    def send_joint(k):
        store(joint, (k,), *joined(k))
        joint_copy(k).start()

    attend(0, 0)
    for k in range(1, groups):
        query_copy(k).wait_recv()
        forward_copy(k).start()
        if k >= 2:
            serve_partner(k - 1)
        attend(k, 0)
        if k >= 3:
            send_joint(k - 2)
    serve_partner(groups - 1)
    serve_partner(0)
    for k in range(max(1, groups - 2), groups):
        send_joint(k)
    running = joined(0)
    for k in range(1, groups):
        joint_copy(k).wait_recv()
        running = join(running, load(got, (k,)))
    latent_out = (running[2] / running[1]).astype(jnp.bfloat16).astype(jnp.float32)
    for c in range(LATENT // LANES):
        lat[c] = latent_out[:, c * LANES:(c + 1) * LANES]

    loads[2].wait()
    for h in range(heads):
        pick = pl.ds(h, steps, stride=heads)
        row = jnp.concatenate([lat[c, pick, :] for c in range(LATENT // LANES)], axis=1)
        hf[pick, :] = jnp.dot(
            row.astype(jnp.bfloat16), wv[h], preferred_element_type=jnp.float32
        )
    hsend[...] = hf[...].astype(jnp.bfloat16)
    for e in range(1, n_req):
        head_copy(e).start()
    hall[req] = hsend[...]
    for e in range(1, n_req):
        head_copy(e).wait_recv()
    for r in range(n_req):
        hwide[r * rows:(r + 1) * rows, :] = hall[r].astype(jnp.float32)
    flat = jnp.concatenate(
        [hwide[pl.ds(h, n_req * steps, stride=heads), :] for h in range(heads)], axis=1
    ).astype(jnp.bfloat16)

    loads[3].wait()
    mixed = jnp.dot(flat, wo[...], preferred_element_type=jnp.float32)
    for j in range(n_seq):
        ysend[j] = mixed[:, j * cols:(j + 1) * cols].astype(jnp.bfloat16)
    for d in order:
        out_copy(d).start()
    total = ysend[me].astype(jnp.float32)
    for d in order:
        out_copy(d).wait_recv()
        total = total + yrecv[d].astype(jnp.float32)
    out_ref[...] = total

    for k in range(groups):
        forward_copy(k).wait_send()
        pair_copy(k).wait_send()
    for k in range(1, groups):
        query_copy(k).wait_send()
        joint_copy(k).wait_send()
    for d in order:
        out_copy(d).wait_send()
    for e in range(1, n_req):
        head_copy(e).wait_send()


def body(n_seq, n_req, latent_cache, queries, chosen, position, w_value, w_out):
    req_dev, cache_len, width = latent_cache.shape
    assert req_dev == 1
    steps, heads = queries.shape[1], queries.shape[2]
    rows = steps * heads
    groups = n_seq // 2
    assert n_seq == 2 * groups and groups & (groups - 1) == 0
    vdim = w_value.shape[2]
    cols = w_out.shape[1] // n_seq
    bf16, f32 = jnp.bfloat16, jnp.float32
    everywhere = pl.BlockSpec(memory_space=pl.ANY)
    scalars = pl.BlockSpec(memory_space=pltpu.SMEM)
    dma = pltpu.SemaphoreType.DMA
    mixed_out = pl.pallas_call(
        functools.partial(kernel, n_seq, n_req, steps, heads),
        out_shape=jax.ShapeDtypeStruct((n_req * steps, cols), f32),
        in_specs=[scalars, scalars] + [everywhere] * 4,
        out_specs=pl.BlockSpec(memory_space=pltpu.VMEM),
        scratch_shapes=[
            pltpu.VMEM((groups, 2, rows, width), bf16),
            pltpu.VMEM((width, cache_len), bf16),
            pltpu.VMEM(w_value.shape, bf16),
            pltpu.VMEM(w_out.shape, bf16),
            pltpu.VMEM((rows, cache_len), f32),
            pltpu.VMEM((groups, 2, rows, LATENT + STATS), bf16),
            pltpu.VMEM((groups, rows, LATENT + STATS), bf16),
            pltpu.VMEM((groups, rows, LATENT + STATS), bf16),
            pltpu.VMEM((groups, rows, LATENT + STATS), bf16),
            pltpu.VMEM((LATENT // LANES, rows, LANES), f32),
            pltpu.VMEM((rows, vdim), f32),
            pltpu.VMEM((rows, vdim), bf16),
            pltpu.VMEM((n_req, rows, vdim), bf16),
            pltpu.VMEM((n_req * rows, vdim), f32),
            pltpu.VMEM((n_seq, n_req * steps, cols), bf16),
            pltpu.VMEM((n_seq, n_req * steps, cols), bf16),
            dma((4,)),
            dma((groups,)), dma((groups,)), dma((groups,)), dma((groups,)),
            dma((groups,)), dma((groups,)), dma((groups,)), dma((groups,)),
            dma((n_req,)), dma((n_req,)), dma((n_seq,)), dma((n_seq,)),
        ],
        compiler_params=pltpu.CompilerParams(
            collective_id=0, has_side_effects=True, vmem_limit_bytes=60 << 20
        ),
    )(
        chosen.transpose(1, 0, 2),
        position,
        queries.reshape(rows, width),
        latent_cache.reshape(cache_len, width).T,
        w_value,
        w_out,
    )
    return mixed_out.T.astype(bf16)


def solution(mesh):
    return jax.shard_map(
        functools.partial(body, mesh.shape["seq"], mesh.shape["req"]),
        mesh=mesh,
        in_specs=(
            P("req", "seq", None),
            P("req", None, "seq", None),
            P("req", None, None),
            P("req"),
            P("seq", None, None),
            P("seq", "req"),
        ),
        out_specs=P(("req", "seq"), None),
        check_vma=False,
    )
```

```python
import functools
import math

import jax
import jax.numpy as jnp
from jax import lax
from jax.experimental import pallas as pl
from jax.experimental.pallas import tpu as pltpu
from jax.sharding import PartitionSpec as P

LATENT = 512
BLOCK = 64
LANES = 128
HALVES = 2
STATS = 128
MESH = pl.DeviceIdType.MESH

score_scale = 1.0 / math.sqrt(192.0)
very_low = -1e30


def kernel(
    n_seq, n_req, steps, heads,
    chosen_ref, position_ref, q_hbm, cache_hbm, wv_hbm, wo_hbm,
    out_ref,
    own, qbuf, cache, wv, wo, mask, part, pair, joint, got, lat, hf, hsend, hall, hwide, ysend, yrecv,
    load_sem, q_send, q_recv, f_send, f_recv, p_send, p_recv, j_send, j_recv,
    h_send, h_recv, y_send, y_recv,
):
    me = lax.axis_index("seq")
    req = lax.axis_index("req")
    rows = steps * heads
    part_rows = rows // HALVES
    cache_len = cache.shape[1]
    outs, cols = out_ref.shape
    groups = n_seq // 2
    group, side = me // 2, me % 2

    loads = [
        pltpu.make_async_copy(q_hbm, own, load_sem.at[0]),
        pltpu.make_async_copy(cache_hbm, cache, load_sem.at[1]),
        pltpu.make_async_copy(wv_hbm, wv, load_sem.at[2]),
        pltpu.make_async_copy(wo_hbm, wo, load_sem.at[3]),
    ]
    loads[0].start()
    loads[1].start()

    def seq_at(offset):
        return {"seq": lax.rem(me + offset, n_seq)}

    def req_at(offset):
        return {"req": lax.rem(req + offset, n_req)}

    def column(k):
        other, bit = 0, 1
        while bit < groups:
            own = (group // bit) % 2
            other = other + bit * ((1 - own) if k & bit else own)
            bit *= 2
        return {"seq": 2 * other + side}

    partner = {"seq": 2 * group + 1 - side}

    barrier = pltpu.get_barrier_semaphore()
    for d in range(1, n_seq):
        pl.semaphore_signal(barrier, inc=1, device_id=seq_at(d), device_id_type=MESH)
    for e in range(1, n_req):
        pl.semaphore_signal(barrier, inc=1, device_id=req_at(e), device_id_type=MESH)

    block = me * (cache_len // BLOCK) + lax.broadcasted_iota(jnp.int32, (1, cache_len), 1) // BLOCK
    inside = me * cache_len + lax.broadcasted_iota(jnp.int32, (1, cache_len), 1) < position_ref[0]
    row_step = lax.broadcasted_iota(jnp.int32, (rows, cache_len), 0) // heads
    usable = jnp.zeros((rows, cache_len), jnp.float32)
    for t in range(steps):
        named = block == chosen_ref[t, 0, 0]
        for k in range(1, chosen_ref.shape[2]):
            named = named | (block == chosen_ref[t, 0, k])
        flag = jnp.where(named & inside, 1.0, 0.0)
        usable = jnp.where(row_step == t, flag, usable)
    for p in range(HALVES):
        mask[p] = usable[p * part_rows:(p + 1) * part_rows]
    pl.semaphore_wait(barrier, n_seq + n_req - 2)

    def remote(src, dst, send, recv, device):
        return pltpu.make_async_remote_copy(
            src_ref=src, dst_ref=dst, send_sem=send, recv_sem=recv,
            device_id=device, device_id_type=MESH,
        )

    def slot(p, k):
        return p * groups + k

    def query_copy(p, k):
        i = slot(p, k)
        return remote(q_hbm.at[p], qbuf.at[i, 0], q_send.at[i], q_recv.at[i], column(k))

    def forward_copy(p, k):
        i = slot(p, k)
        src = qbuf.at[i, 0] if k else q_hbm.at[p]
        return remote(src, qbuf.at[i, 1], f_send.at[i], f_recv.at[i], partner)

    def pair_copy(p, k):
        i = slot(p, k)
        return remote(part.at[i, 1], pair.at[i], p_send.at[i], p_recv.at[i], partner)

    def joint_copy(p, k):
        i = slot(p, k)
        return remote(joint.at[i], got.at[i], j_send.at[i], j_recv.at[i], column(k))

    def head_copy(e):
        return remote(hsend, hall.at[req], h_send.at[e], h_recv.at[e], req_at(e))

    def out_copy(d):
        return remote(
            ysend.at[lax.rem(me + d, n_seq)], yrecv.at[d], y_send.at[d], y_recv.at[d], seq_at(d)
        )

    order = sorted(range(1, n_seq), key=lambda d: (-min(d, n_seq - d), d))
    for p in range(HALVES):
        forward_copy(p, 0).start()
        for k in range(1, groups):
            query_copy(p, k).start()
    loads[2].start()
    loads[3].start()
    loads[0].wait()
    loads[1].wait()

    def store(ref, at, peak, total, summed):
        high = total.astype(jnp.bfloat16).astype(jnp.float32)
        lane = lax.broadcasted_iota(jnp.int32, (part_rows, STATS), 1)
        stats = jnp.where(lane == 0, peak, jnp.where(lane == 1, high, total - high))
        ref[at + (slice(None), slice(0, LATENT))] = summed.astype(jnp.bfloat16)
        ref[at + (slice(None), slice(LATENT, LATENT + STATS))] = stats.astype(jnp.bfloat16)

    def load(ref, at):
        stats = ref[at + (slice(None), slice(LATENT, LATENT + STATS))].astype(jnp.float32)
        return (
            stats[:, 0:1],
            stats[:, 1:2] + stats[:, 2:3],
            ref[at + (slice(None), slice(0, LATENT))].astype(jnp.float32),
        )

    def attend(p, k, j):
        i = slot(p, k)
        queries = own[p] if (k, j) == (0, 0) else qbuf[i, j]
        keep = mask[p] > 0.0
        scores = lax.dot_general(
            queries, cache[...], (((1,), (0,)), ((), ())), preferred_element_type=jnp.float32
        ) * score_scale
        scores = jnp.where(keep, scores, very_low)
        peak = jnp.max(scores, axis=1, keepdims=True).astype(jnp.bfloat16).astype(jnp.float32)
        raw = jnp.where(keep, jnp.exp(scores - peak), 0.0)
        total = jnp.sum(raw, axis=1, keepdims=True)
        summed = lax.dot_general(
            raw.astype(jnp.bfloat16), cache[:LATENT, :], (((1,), (1,)), ((), ())),
            preferred_element_type=jnp.float32,
        )
        store(part, (i, j), peak, total, summed)

    def join(left, right):
        peak = jnp.maximum(left[0], right[0])
        scale_left = jnp.exp(left[0] - peak)
        scale_right = jnp.exp(right[0] - peak)
        return (
            peak,
            left[1] * scale_left + right[1] * scale_right,
            left[2] * scale_left + right[2] * scale_right,
        )

    def serve_column(p, k):
        query_copy(p, k).wait_recv()
        forward_copy(p, k).start()
        attend(p, k, 0)

    def serve_partner(p, k):
        forward_copy(p, k).wait_recv()
        attend(p, k, 1)
        pair_copy(p, k).start()

    def joined(p, k):
        pair_copy(p, k).wait_recv()
        return join(load(part, (slot(p, k), 0)), load(pair, (slot(p, k),)))

    def send_joint(p, k):
        store(joint, (slot(p, k),), *joined(p, k))
        joint_copy(p, k).start()

    others = range(1, groups)
    for p in range(HALVES):
        attend(p, 0, 0)
    for p in range(HALVES):
        serve_partner(p, 0)
    for k in others:
        serve_column(0, k)
    for p in range(HALVES):
        for k in others:
            if p + 1 < HALVES:
                serve_column(p + 1, k)
            serve_partner(p, k)
            if p:
                send_joint(p - 1, k)
    for k in others:
        send_joint(HALVES - 1, k)
    for p in range(HALVES):
        running = joined(p, 0)
        for k in others:
            joint_copy(p, k).wait_recv()
            running = join(running, load(got, (slot(p, k),)))
        latent_out = (running[2] / running[1]).astype(jnp.bfloat16).astype(jnp.float32)
        for c in range(LATENT // LANES):
            lat[c, p * part_rows:(p + 1) * part_rows, :] = (
                latent_out[:, c * LANES:(c + 1) * LANES]
            )

    loads[2].wait()
    for h in range(heads):
        pick = pl.ds(h, steps, stride=heads)
        row = jnp.concatenate([lat[c, pick, :] for c in range(LATENT // LANES)], axis=1)
        hf[pick, :] = jnp.dot(
            row.astype(jnp.bfloat16), wv[h], preferred_element_type=jnp.float32
        )
    hsend[...] = hf[...].astype(jnp.bfloat16)
    for e in range(1, n_req):
        head_copy(e).start()
    hall[req] = hsend[...]
    for e in range(1, n_req):
        head_copy(e).wait_recv()
    for r in range(n_req):
        hwide[r * rows:(r + 1) * rows, :] = hall[r].astype(jnp.float32)
    flat = jnp.concatenate(
        [hwide[pl.ds(h, n_req * steps, stride=heads), :] for h in range(heads)], axis=1
    ).astype(jnp.bfloat16)

    loads[3].wait()
    mixed = jnp.dot(flat, wo[...], preferred_element_type=jnp.float32)
    for j in range(n_seq):
        ysend[j, :outs, :cols] = mixed[:, j * cols:(j + 1) * cols].astype(jnp.bfloat16)
    for d in order:
        out_copy(d).start()
    total = ysend[me].astype(jnp.float32)
    for d in order:
        out_copy(d).wait_recv()
        total = total + yrecv[d].astype(jnp.float32)
    out_ref[...] = total[:outs, :cols]

    for p in range(HALVES):
        for k in range(groups):
            forward_copy(p, k).wait_send()
            pair_copy(p, k).wait_send()
        for k in others:
            query_copy(p, k).wait_send()
            joint_copy(p, k).wait_send()
    for d in order:
        out_copy(d).wait_send()
    for e in range(1, n_req):
        head_copy(e).wait_send()


def body(n_seq, n_req, latent_cache, queries, chosen, position, w_value, w_out):
    req_dev, cache_len, width = latent_cache.shape
    assert req_dev == 1
    steps, heads = queries.shape[1], queries.shape[2]
    rows = steps * heads
    groups = n_seq // 2
    slots, part_rows = HALVES * groups, rows // HALVES
    assert rows == HALVES * part_rows
    assert n_seq == 2 * groups and groups & (groups - 1) == 0
    vdim = w_value.shape[2]
    cols = w_out.shape[1] // n_seq
    out_rows = -(-n_req * steps // 16) * 16
    out_lanes = -(-cols // LANES) * LANES
    bf16, f32 = jnp.bfloat16, jnp.float32
    everywhere = pl.BlockSpec(memory_space=pl.ANY)
    scalars = pl.BlockSpec(memory_space=pltpu.SMEM)
    dma = pltpu.SemaphoreType.DMA
    mixed_out = pl.pallas_call(
        functools.partial(kernel, n_seq, n_req, steps, heads),
        out_shape=jax.ShapeDtypeStruct((n_req * steps, cols), f32),
        in_specs=[scalars, scalars] + [everywhere] * 4,
        out_specs=pl.BlockSpec(memory_space=pltpu.VMEM),
        scratch_shapes=[
            pltpu.VMEM((HALVES, part_rows, width), bf16),
            pltpu.VMEM((slots, 2, part_rows, width), bf16),
            pltpu.VMEM((width, cache_len), bf16),
            pltpu.VMEM(w_value.shape, bf16),
            pltpu.VMEM(w_out.shape, bf16),
            pltpu.VMEM((HALVES, part_rows, cache_len), f32),
            pltpu.VMEM((slots, 2, part_rows, LATENT + STATS), bf16),
            pltpu.VMEM((slots, part_rows, LATENT + STATS), bf16),
            pltpu.VMEM((slots, part_rows, LATENT + STATS), bf16),
            pltpu.VMEM((slots, part_rows, LATENT + STATS), bf16),
            pltpu.VMEM((LATENT // LANES, rows, LANES), f32),
            pltpu.VMEM((rows, vdim), f32),
            pltpu.VMEM((rows, vdim), bf16),
            pltpu.VMEM((n_req, rows, vdim), bf16),
            pltpu.VMEM((n_req * rows, vdim), f32),
            pltpu.VMEM((n_seq, out_rows, out_lanes), bf16),
            pltpu.VMEM((n_seq, out_rows, out_lanes), bf16),
            dma((4,)),
            dma((slots,)), dma((slots,)), dma((slots,)), dma((slots,)),
            dma((slots,)), dma((slots,)), dma((slots,)), dma((slots,)),
            dma((n_req,)), dma((n_req,)), dma((n_seq,)), dma((n_seq,)),
        ],
        compiler_params=pltpu.CompilerParams(
            collective_id=0, has_side_effects=True, vmem_limit_bytes=60 << 20
        ),
    )(
        chosen.transpose(1, 0, 2),
        position,
        queries.reshape(HALVES, part_rows, width),
        latent_cache.reshape(cache_len, width).T,
        w_value,
        w_out,
    )
    return mixed_out.T.astype(bf16)


def solution(mesh):
    return jax.shard_map(
        functools.partial(body, mesh.shape["seq"], mesh.shape["req"]),
        mesh=mesh,
        in_specs=(
            P("req", "seq", None),
            P("req", None, "seq", None),
            P("req", None, None),
            P("req"),
            P("seq", None, None),
            P("seq", "req"),
        ),
        out_specs=P(("req", "seq"), None),
        check_vma=False,
    )
```

```python
import functools
import math

import jax
import jax.numpy as jnp
from jax import lax
from jax.experimental import pallas as pl
from jax.experimental.pallas import tpu as pltpu
from jax.sharding import PartitionSpec as P

LATENT = 512
BLOCK = 64
LANES = 128
HALVES = 1
STATS = 128
MESH = pl.DeviceIdType.MESH

score_scale = 1.0 / math.sqrt(192.0)
very_low = -1e30


def kernel(
    n_seq, n_req, steps, heads,
    chosen_ref, position_ref, q_hbm, cache_hbm, wv_hbm, wo_hbm,
    out_ref,
    own, qbuf, cache, wv, wo, mask, part, pair, joint, got, lat, hf, hsend, hall, hwide, ysend, yrecv,
    load_sem, q_send, q_recv, f_send, f_recv, p_send, p_recv, j_send, j_recv,
    h_send, h_recv, y_send, y_recv,
):
    me = lax.axis_index("seq")
    req = lax.axis_index("req")
    rows = steps * heads
    part_rows = rows // HALVES
    cache_len = cache.shape[1]
    outs, cols = out_ref.shape
    groups = n_seq // 2
    group, side = me // 2, me % 2

    loads = [
        pltpu.make_async_copy(q_hbm, own, load_sem.at[0]),
        pltpu.make_async_copy(cache_hbm, cache, load_sem.at[1]),
        pltpu.make_async_copy(wv_hbm, wv, load_sem.at[2]),
        pltpu.make_async_copy(wo_hbm, wo, load_sem.at[3]),
    ]
    loads[0].start()
    loads[1].start()

    def seq_at(offset):
        return {"seq": lax.rem(me + offset, n_seq)}

    def req_at(offset):
        return {"req": lax.rem(req + offset, n_req)}

    def column(k):
        other, bit = 0, 1
        while bit < groups:
            own = (group // bit) % 2
            other = other + bit * ((1 - own) if k & bit else own)
            bit *= 2
        return {"seq": 2 * other + side}

    partner = {"seq": 2 * group + 1 - side}

    barrier = pltpu.get_barrier_semaphore()
    for d in range(1, n_seq):
        pl.semaphore_signal(barrier, inc=1, device_id=seq_at(d), device_id_type=MESH)
    for e in range(1, n_req):
        pl.semaphore_signal(barrier, inc=1, device_id=req_at(e), device_id_type=MESH)

    block = me * (cache_len // BLOCK) + lax.broadcasted_iota(jnp.int32, (1, cache_len), 1) // BLOCK
    inside = me * cache_len + lax.broadcasted_iota(jnp.int32, (1, cache_len), 1) < position_ref[0]
    row_step = lax.broadcasted_iota(jnp.int32, (rows, cache_len), 0) // heads
    usable = jnp.zeros((rows, cache_len), jnp.float32)
    for t in range(steps):
        named = block == chosen_ref[t, 0, 0]
        for k in range(1, chosen_ref.shape[2]):
            named = named | (block == chosen_ref[t, 0, k])
        flag = jnp.where(named & inside, 1.0, 0.0)
        usable = jnp.where(row_step == t, flag, usable)
    for p in range(HALVES):
        mask[p] = usable[p * part_rows:(p + 1) * part_rows]
    pl.semaphore_wait(barrier, n_seq + n_req - 2)

    def remote(src, dst, send, recv, device):
        return pltpu.make_async_remote_copy(
            src_ref=src, dst_ref=dst, send_sem=send, recv_sem=recv,
            device_id=device, device_id_type=MESH,
        )

    def slot(p, k):
        return p * groups + k

    def query_copy(p, k):
        i = slot(p, k)
        return remote(q_hbm.at[p], qbuf.at[i, 0], q_send.at[i], q_recv.at[i], column(k))

    def forward_copy(p, k):
        i = slot(p, k)
        src = qbuf.at[i, 0] if k else q_hbm.at[p]
        return remote(src, qbuf.at[i, 1], f_send.at[i], f_recv.at[i], partner)

    def pair_copy(p, k):
        i = slot(p, k)
        return remote(part.at[i, 1], pair.at[i], p_send.at[i], p_recv.at[i], partner)

    def joint_copy(p, k):
        i = slot(p, k)
        return remote(joint.at[i], got.at[i], j_send.at[i], j_recv.at[i], column(k))

    def head_copy(e):
        return remote(hsend, hall.at[req], h_send.at[e], h_recv.at[e], req_at(e))

    def out_copy(d):
        return remote(
            ysend.at[lax.rem(me + d, n_seq)], yrecv.at[d], y_send.at[d], y_recv.at[d], seq_at(d)
        )

    order = sorted(range(1, n_seq), key=lambda d: (-min(d, n_seq - d), d))
    for p in range(HALVES):
        forward_copy(p, 0).start()
        for k in range(1, groups):
            query_copy(p, k).start()
    loads[2].start()
    loads[3].start()
    loads[0].wait()
    loads[1].wait()

    def store(ref, at, peak, total, summed):
        high = total.astype(jnp.bfloat16).astype(jnp.float32)
        lane = lax.broadcasted_iota(jnp.int32, (part_rows, STATS), 1)
        stats = jnp.where(lane == 0, peak, jnp.where(lane == 1, high, total - high))
        ref[at + (slice(None), slice(0, LATENT))] = summed.astype(jnp.bfloat16)
        ref[at + (slice(None), slice(LATENT, LATENT + STATS))] = stats.astype(jnp.bfloat16)

    def load(ref, at):
        stats = ref[at + (slice(None), slice(LATENT, LATENT + STATS))].astype(jnp.float32)
        return (
            stats[:, 0:1],
            stats[:, 1:2] + stats[:, 2:3],
            ref[at + (slice(None), slice(0, LATENT))].astype(jnp.float32),
        )

    def attend(p, k, j):
        i = slot(p, k)
        queries = own[p] if (k, j) == (0, 0) else qbuf[i, j]
        keep = mask[p] > 0.0
        scores = lax.dot_general(
            queries, cache[...], (((1,), (0,)), ((), ())), preferred_element_type=jnp.float32
        ) * score_scale
        scores = jnp.where(keep, scores, very_low)
        peak = jnp.max(scores, axis=1, keepdims=True).astype(jnp.bfloat16).astype(jnp.float32)
        raw = jnp.where(keep, jnp.exp(scores - peak), 0.0)
        total = jnp.sum(raw, axis=1, keepdims=True)
        summed = lax.dot_general(
            raw.astype(jnp.bfloat16), cache[:LATENT, :], (((1,), (1,)), ((), ())),
            preferred_element_type=jnp.float32,
        )
        store(part, (i, j), peak, total, summed)

    def join(left, right):
        peak = jnp.maximum(left[0], right[0])
        scale_left = jnp.exp(left[0] - peak)
        scale_right = jnp.exp(right[0] - peak)
        return (
            peak,
            left[1] * scale_left + right[1] * scale_right,
            left[2] * scale_left + right[2] * scale_right,
        )

    def serve_column(p, k):
        query_copy(p, k).wait_recv()
        forward_copy(p, k).start()
        attend(p, k, 0)

    def serve_partner(p, k):
        forward_copy(p, k).wait_recv()
        attend(p, k, 1)
        pair_copy(p, k).start()

    def joined(p, k):
        pair_copy(p, k).wait_recv()
        return join(load(part, (slot(p, k), 0)), load(pair, (slot(p, k),)))

    def send_joint(p, k):
        store(joint, (slot(p, k),), *joined(p, k))
        joint_copy(p, k).start()

    others = range(1, groups)
    for p in range(HALVES):
        attend(p, 0, 0)
    for p in range(HALVES):
        serve_partner(p, 0)
    for k in others:
        serve_column(0, k)
    for p in range(HALVES):
        for k in others:
            if p + 1 < HALVES:
                serve_column(p + 1, k)
            serve_partner(p, k)
            if p:
                send_joint(p - 1, k)
            elif HALVES == 1 and k > 1:
                send_joint(0, k - 1)
    for k in others if HALVES > 1 else others[-1:]:
        send_joint(HALVES - 1, k)
    for p in range(HALVES):
        running = joined(p, 0)
        for k in others:
            joint_copy(p, k).wait_recv()
            running = join(running, load(got, (slot(p, k),)))
        latent_out = (running[2] / running[1]).astype(jnp.bfloat16).astype(jnp.float32)
        for c in range(LATENT // LANES):
            lat[c, p * part_rows:(p + 1) * part_rows, :] = (
                latent_out[:, c * LANES:(c + 1) * LANES]
            )

    loads[2].wait()
    for h in range(heads):
        pick = pl.ds(h, steps, stride=heads)
        row = jnp.concatenate([lat[c, pick, :] for c in range(LATENT // LANES)], axis=1)
        hf[pick, :] = jnp.dot(
            row.astype(jnp.bfloat16), wv[h], preferred_element_type=jnp.float32
        )
    hsend[...] = hf[...].astype(jnp.bfloat16)
    for e in range(1, n_req):
        head_copy(e).start()
    hall[req] = hsend[...]
    for e in range(1, n_req):
        head_copy(e).wait_recv()
    for r in range(n_req):
        hwide[r * rows:(r + 1) * rows, :] = hall[r].astype(jnp.float32)
    flat = jnp.concatenate(
        [hwide[pl.ds(h, n_req * steps, stride=heads), :] for h in range(heads)], axis=1
    ).astype(jnp.bfloat16)

    loads[3].wait()
    mixed = jnp.dot(flat, wo[...], preferred_element_type=jnp.float32)
    for j in range(n_seq):
        ysend[j, :outs, :cols] = mixed[:, j * cols:(j + 1) * cols].astype(jnp.bfloat16)
    for d in order:
        out_copy(d).start()
    total = ysend[me].astype(jnp.float32)
    for d in order:
        out_copy(d).wait_recv()
        total = total + yrecv[d].astype(jnp.float32)
    out_ref[...] = total[:outs, :cols]

    for p in range(HALVES):
        for k in range(groups):
            forward_copy(p, k).wait_send()
            pair_copy(p, k).wait_send()
        for k in others:
            query_copy(p, k).wait_send()
            joint_copy(p, k).wait_send()
    for d in order:
        out_copy(d).wait_send()
    for e in range(1, n_req):
        head_copy(e).wait_send()


def body(n_seq, n_req, latent_cache, queries, chosen, position, w_value, w_out):
    req_dev, cache_len, width = latent_cache.shape
    assert req_dev == 1
    steps, heads = queries.shape[1], queries.shape[2]
    rows = steps * heads
    groups = n_seq // 2
    slots, part_rows = HALVES * groups, rows // HALVES
    assert rows == HALVES * part_rows
    assert n_seq == 2 * groups and groups & (groups - 1) == 0
    vdim = w_value.shape[2]
    cols = w_out.shape[1] // n_seq
    out_rows = -(-n_req * steps // 16) * 16
    out_lanes = -(-cols // LANES) * LANES
    bf16, f32 = jnp.bfloat16, jnp.float32
    everywhere = pl.BlockSpec(memory_space=pl.ANY)
    scalars = pl.BlockSpec(memory_space=pltpu.SMEM)
    dma = pltpu.SemaphoreType.DMA
    mixed_out = pl.pallas_call(
        functools.partial(kernel, n_seq, n_req, steps, heads),
        out_shape=jax.ShapeDtypeStruct((n_req * steps, cols), f32),
        in_specs=[scalars, scalars] + [everywhere] * 4,
        out_specs=pl.BlockSpec(memory_space=pltpu.VMEM),
        scratch_shapes=[
            pltpu.VMEM((HALVES, part_rows, width), bf16),
            pltpu.VMEM((slots, 2, part_rows, width), bf16),
            pltpu.VMEM((width, cache_len), bf16),
            pltpu.VMEM(w_value.shape, bf16),
            pltpu.VMEM(w_out.shape, bf16),
            pltpu.VMEM((HALVES, part_rows, cache_len), f32),
            pltpu.VMEM((slots, 2, part_rows, LATENT + STATS), bf16),
            pltpu.VMEM((slots, part_rows, LATENT + STATS), bf16),
            pltpu.VMEM((slots, part_rows, LATENT + STATS), bf16),
            pltpu.VMEM((slots, part_rows, LATENT + STATS), bf16),
            pltpu.VMEM((LATENT // LANES, rows, LANES), f32),
            pltpu.VMEM((rows, vdim), f32),
            pltpu.VMEM((rows, vdim), bf16),
            pltpu.VMEM((n_req, rows, vdim), bf16),
            pltpu.VMEM((n_req * rows, vdim), f32),
            pltpu.VMEM((n_seq, out_rows, out_lanes), bf16),
            pltpu.VMEM((n_seq, out_rows, out_lanes), bf16),
            dma((4,)),
            dma((slots,)), dma((slots,)), dma((slots,)), dma((slots,)),
            dma((slots,)), dma((slots,)), dma((slots,)), dma((slots,)),
            dma((n_req,)), dma((n_req,)), dma((n_seq,)), dma((n_seq,)),
        ],
        compiler_params=pltpu.CompilerParams(
            collective_id=0, has_side_effects=True, vmem_limit_bytes=60 << 20
        ),
    )(
        chosen.transpose(1, 0, 2),
        position,
        queries.reshape(HALVES, part_rows, width),
        latent_cache.reshape(cache_len, width).T,
        w_value,
        w_out,
    )
    return mixed_out.T.astype(bf16)


def solution(mesh):
    return jax.shard_map(
        functools.partial(body, mesh.shape["seq"], mesh.shape["req"]),
        mesh=mesh,
        in_specs=(
            P("req", "seq", None),
            P("req", None, "seq", None),
            P("req", None, None),
            P("req"),
            P("seq", None, None),
            P("seq", "req"),
        ),
        out_specs=P(("req", "seq"), None),
        check_vma=False,
    )
```
